128 devices in a mesh: slab: 8 (over y_hi, x), line: 16 (over z, y_lo, core).
Axes of the slice: x: 4, y: 4 (y_hi: 2, y_lo: 2; y = y_hi * 2 + y_lo), z: 4, core: 2. Of those that a mesh axis runs over, the one named last changes fastest.
Arguments:
- estimate: float32 [256, 256, 256], P('slab', 'line'), may hold values from -6 to 6
- support_lo: int32 [256, 256], P('slab', 'line'), may hold values from 0 to 63
- support_hi: int32 [256, 256], P('slab', 'line'), may hold values from 193 to 256
- measured: bfloat16 [2, 2, 512, 512, 2, 128], P(None, None, None, ('slab', 'line')), may hold values from -3 to 3
- blocks: int32 [512, 2, 2], replicated, may hold values from 0 to 3, all different within a row
- wedge: int32 [2], replicated, may hold values from 0 to 511
Outputs:
- updated: float32 [256, 256, 256], P('slab', 'line')
The draws below stay inside these ranges and needn't reach their ends.
Inputs may be any that keep to these rules, and one draw needn't show every extreme that they name: The 2 entries of blocks for one plane frequency and group are distinct.
All inputs are finite; a program needn't handle non-finite values.
Results may differ from the reference program's by a relative error of at most 0.0071.
Values may be sent and summed in bfloat16 or wider, within the bound.
A program may use at most 128 MiB of HBM per device.

```python
import math
import jax
import jax.numpy as jnp
from jax import lax

N = 512
LBLK = 128
MB = 2
OBJ = 256


def with_ends(result, own_key, least, high):
    longest = result.shape.index(max(result.shape))
    spots = []
    for shift in (0, 1):
        where = [jax.random.randint(jax.random.fold_in(own_key, axis), (), 0, length) for axis, length in enumerate(result.shape)]
        where[longest] = (where[longest] + shift) % result.shape[longest]
        spots.append(tuple(where))
    return result.at[spots[0]].set(least).at[spots[1]].set(high)


def level_of(stream_key, dims, split, least, largest):
    level, own = 1.0, jax.random.fold_in(stream_key, 6)
    for dim, parts in split:
        heights = jnp.exp(jax.random.uniform(jax.random.fold_in(own, dim), (parts,), jnp.float32, least / len(split), largest / len(split)))
        level = level * jnp.repeat(heights, dims[dim] // parts).reshape([-1 if axis == dim else 1 for axis in range(len(dims))])
    return level


def choose_distinct(own_key, rows, number_of, top, lift):
    sequence = jax.random.permutation(jax.random.fold_in(own_key, 1), number_of)
    pull = sequence
    for power in range(3):
        pull = pull * pull // number_of
    pull = pull * lift // number_of
    lots = jax.random.randint(jax.random.fold_in(own_key, 2), (rows, number_of), 0, 4096) + pull
    holders = jax.random.permutation(jax.random.fold_in(own_key, 3), rows)[jnp.arange(number_of) % rows]
    lots = jnp.where(jnp.arange(rows)[:, None] == holders[None, :], 1 << 14, lots)
    priority = lots * number_of + jnp.arange(number_of)
    return lax.top_k(priority.astype(jnp.int32), top)[1].astype(jnp.int32)


def centred(stream_key, shape, spread, bound, pieces=(), held_as=jnp.bfloat16):
    result = spread * jax.random.normal(stream_key, shape, jnp.float32)
    if pieces:
        result = result * level_of(stream_key, shape, pieces, -0.22, 0.18)
    return jnp.clip(result, -bound, bound).astype(held_as)


def setup_inputs(seed: int = 0) -> dict:
    key_of = jax.random.split(jax.random.key(seed), 7)
    return {
        "estimate": centred(key_of[0], (OBJ, OBJ, OBJ), 1.0, 6.0, ((0, 8), (1, 16)), jnp.float32),
        "support_lo": with_ends(jax.random.randint(key_of[1], (OBJ, OBJ), 0, OBJ // 4), jax.random.fold_in(key_of[1], 1), 0, (OBJ // 4) - 1).astype(jnp.int32),
        "support_hi": with_ends(jax.random.randint(key_of[2], (OBJ, OBJ), 3 * OBJ // 4 + 1, OBJ + 1), jax.random.fold_in(key_of[2], 1), 3 * OBJ // 4 + 1, OBJ).astype(jnp.int32),
        "measured": centred(key_of[3], (2, 2, N, N, MB, LBLK), 0.5, 3.0, ((3, 128),)),
        "blocks": choose_distinct(key_of[4], N * 2, N // LBLK, MB, 0).reshape((N, 2, MB)),
        "wedge": jax.random.randint(key_of[5], (2,), 0, N).astype(jnp.int32),
    }


def phase_table(left_int, right_int, period):
    product = jnp.mod(left_int * right_int, period)
    angle = product.astype(jnp.float32) * (2.0 * math.pi / period)
    factor = 1.0 / math.sqrt(N)
    return ((jnp.cos(angle) * factor).astype(jnp.bfloat16), (jnp.sin(angle) * factor).astype(jnp.bfloat16))

def product_single_precision(form, left_op, right_op):
    return jnp.einsum(form, left_op.astype(jnp.float32), right_op.astype(jnp.float32))

def reference(estimate, support_lo, support_hi, measured, blocks, wedge):
    half_freq = N // 2
    nblocks = N // LBLK
    freq_coord = jnp.arange(N, dtype=jnp.int32) - half_freq
    cell_coord = jnp.arange(OBJ, dtype=jnp.int32) - OBJ // 2
    dft_cos, dft_sin = phase_table(freq_coord[:, None], cell_coord[None, :], N)
    cells = estimate.astype(jnp.bfloat16)
    spec_are = product_single_precision('kx,zxy->zky', dft_cos, cells).astype(jnp.bfloat16)
    spec_aim = (-product_single_precision('kx,zxy->zky', dft_sin, cells)).astype(jnp.bfloat16)
    spec_bre = product_single_precision('ky,zxy->zkx', dft_cos, cells).astype(jnp.bfloat16)
    spec_bim = (-product_single_precision('ky,zxy->zkx', dft_sin, cells)).astype(jnp.bfloat16)
    spectrum = jnp.stack([jnp.stack([spec_are, spec_aim]), jnp.stack([spec_bre, spec_bim])])
    weights = (jnp.abs(freq_coord).astype(jnp.float32) + 1.0) / half_freq
    low_end = jnp.minimum(wedge[0], wedge[1])
    high_end = jnp.maximum(wedge[0], wedge[1])
    line_index = jnp.arange(N, dtype=jnp.int32)
    excluded = ((line_index >= low_end) & (line_index < high_end)).reshape(nblocks, LBLK)
    indicator_matrix = (blocks[:, :, :, None] == jnp.arange(nblocks, dtype=jnp.int32)).astype(jnp.float32)
    covered = jnp.any(blocks[:, :, :, None] == jnp.arange(nblocks, dtype=jnp.int32), axis=2)
    usable = jnp.transpose(covered, (1, 0, 2))[:, :, None, :, None] & (~excluded)[None, None, None, :, :]
    tile_row_count = 32

    def step(total, block_index):
        offset_position = (block_index * tile_row_count).astype(jnp.int32)
        piece = lax.dynamic_slice_in_dim(spectrum, offset_position, tile_row_count, 3)
        pen_re = (product_single_precision('az,gzkc->gakc', dft_cos, piece[:, 0]) + product_single_precision('az,gzkc->gakc', dft_sin, piece[:, 1])).astype(jnp.bfloat16)
        pen_im = (product_single_precision('az,gzkc->gakc', dft_cos, piece[:, 1]) - product_single_precision('az,gzkc->gakc', dft_sin, piece[:, 0])).astype(jnp.bfloat16)
        kvalues = lax.dynamic_slice_in_dim(freq_coord, offset_position, tile_row_count, 0)
        frac_cos, frac_sin = phase_table((2 * kvalues)[:, None, None] * freq_coord[None, :, None], cell_coord[None, None, :], N * N)
        polar_re = product_single_precision('klc,gakc->gakl', frac_cos, pen_re) + product_single_precision('klc,gakc->gakl', frac_sin, pen_im)
        polar_im = product_single_precision('klc,gakc->gakl', frac_cos, pen_im) - product_single_precision('klc,gakc->gakl', frac_sin, pen_re)
        measurement_tile = lax.dynamic_slice_in_dim(measured, offset_position, tile_row_count, 3)
        overwritten_result = product_single_precision('voef,ozvnei->ozvnfi', indicator_matrix, measurement_tile)
        shape_five = (2, N, tile_row_count, nblocks, LBLK)
        kweight = lax.dynamic_slice_in_dim(weights, offset_position, tile_row_count, 0)[None, None, :, None, None]
        sub_re = jnp.where(usable, overwritten_result[:, 0], polar_re.reshape(shape_five)) * kweight
        difference_imaginary = jnp.where(usable, overwritten_result[:, 1], polar_im.reshape(shape_five)) * kweight
        weighted_re = sub_re.reshape(2, N, tile_row_count, N).astype(jnp.bfloat16)
        weighted_im = difference_imaginary.reshape(2, N, tile_row_count, N).astype(jnp.bfloat16)
        adj_re = (product_single_precision('klc,gakl->gakc', frac_cos, weighted_re) - product_single_precision('klc,gakl->gakc', frac_sin, weighted_im)).astype(jnp.bfloat16)
        adj_im = (product_single_precision('klc,gakl->gakc', frac_cos, weighted_im) + product_single_precision('klc,gakl->gakc', frac_sin, weighted_re)).astype(jnp.bfloat16)
        plan_re = (product_single_precision('az,gakc->gzkc', dft_cos, adj_re) - product_single_precision('az,gakc->gzkc', dft_sin, adj_im)).astype(jnp.bfloat16)
        plan_im = (product_single_precision('az,gakc->gzkc', dft_cos, adj_im) + product_single_precision('az,gakc->gzkc', dft_sin, adj_re)).astype(jnp.bfloat16)
        rows_cos = lax.dynamic_slice_in_dim(dft_cos, offset_position, tile_row_count, 0)
        rows_sin = lax.dynamic_slice_in_dim(dft_sin, offset_position, tile_row_count, 0)
        image = product_single_precision('kx,zky->zxy', rows_cos, plan_re[0]) - product_single_precision('kx,zky->zxy', rows_sin, plan_im[0])
        image = image + product_single_precision('ky,zkx->zxy', rows_cos, plan_re[1]) - product_single_precision('ky,zkx->zxy', rows_sin, plan_im[1])
        return (total + image, None)
    total, _ = lax.scan(step, jnp.zeros((OBJ, OBJ, OBJ), jnp.float32), jnp.arange(N // tile_row_count, dtype=jnp.int32))
    ycoord = jnp.arange(OBJ, dtype=jnp.int32)
    inside = (ycoord[None, None, :] >= support_lo[:, :, None]) & (ycoord[None, None, :] < support_hi[:, :, None])
    return jnp.where(inside & (total > 0.0), total, jnp.float32(0.0))
```

```python
import math

import jax
import jax.numpy as jnp
from jax import lax
from jax.sharding import PartitionSpec as P

N = 512


def phase_table(left_int, right_int, period):
    product = jnp.mod(left_int * right_int, period)
    angle = product.astype(jnp.float32) * (2.0 * math.pi / period)
    factor = 1.0 / math.sqrt(N)
    return (
        (jnp.cos(angle) * factor).astype(jnp.bfloat16),
        (jnp.sin(angle) * factor).astype(jnp.bfloat16),
    )


def contract(form, left_op, right_op):
    return jnp.einsum(form, left_op, right_op, preferred_element_type=jnp.float32)


def shards(estimate, support_lo, support_hi, measured, blocks, wedge):
    slab_count = lax.axis_size("slab")
    line_count = lax.axis_size("line")
    slab_index = lax.axis_index("slab")
    line_index = lax.axis_index("line")
    plane_rows, row_count, obj_len = estimate.shape
    half_freq = N // 2
    per_line = N // line_count
    per_device = per_line // slab_count
    per_slab = N // slab_count
    cell_coord = jnp.arange(obj_len, dtype=jnp.int32) - obj_len // 2
    local_order = jnp.arange(per_line, dtype=jnp.int32)
    plane_freq = (
        local_order // per_device * per_slab + line_index * per_device + local_order % per_device
    )
    own_freq = (
        slab_index * per_slab + line_index * per_device + jnp.arange(per_device, dtype=jnp.int32)
    )
    all_freq = jnp.arange(N, dtype=jnp.int32) - half_freq
    back_order = jnp.arange(N, dtype=jnp.int32)
    back_freq = (
        (back_order // per_line) * per_device
        + ((back_order % per_line) // per_device) * per_slab
        + back_order % per_device
    )
    tables = (
        phase_table((plane_freq - half_freq)[:, None], cell_coord[None, :], N)
        + phase_table(all_freq[:, None], cell_coord[None, :], N)
        + phase_table(
            (2 * (own_freq - half_freq))[:, None, None] * all_freq[None, :, None],
            cell_coord[None, None, :],
            N * N,
        )
        + phase_table((back_freq - half_freq)[:, None], cell_coord[None, :], N)
    )
    (plane_cos, plane_sin, dz_cos, dz_sin, frac_cos, frac_sin, back_cos, back_sin) = (
        lax.optimization_barrier(tables)
    )

    cells = estimate.astype(jnp.bfloat16)
    piece = lax.all_gather(cells, "line", axis=1, tiled=True)
    real_a = contract("kx,zxy->zky", plane_cos, piece)
    imag_a = -contract("kx,zxy->zky", plane_sin, piece)
    real_b = contract("ky,zxy->zkx", plane_cos, piece)
    imag_b = -contract("ky,zxy->zkx", plane_sin, piece)
    spectrum = jnp.stack([jnp.stack([real_a, imag_a]), jnp.stack([real_b, imag_b])]).astype(
        jnp.bfloat16
    )
    gathered = lax.all_to_all(spectrum, "slab", split_axis=3, concat_axis=2, tiled=True)
    pen_re = (
        contract("az,gzkc->gakc", dz_cos, gathered[:, 0])
        + contract("az,gzkc->gakc", dz_sin, gathered[:, 1])
    ).astype(jnp.bfloat16)
    pen_im = (
        contract("az,gzkc->gakc", dz_cos, gathered[:, 1])
        - contract("az,gzkc->gakc", dz_sin, gathered[:, 0])
    ).astype(jnp.bfloat16)
    polar_re = contract("klc,gakc->gakl", frac_cos, pen_re) + contract(
        "klc,gakc->gakl", frac_sin, pen_im
    )
    polar_im = contract("klc,gakc->gakl", frac_cos, pen_im) - contract(
        "klc,gakc->gakl", frac_sin, pen_re
    )
    block_len = measured.shape[-1]
    nblocks = N // block_len
    block_ids = jnp.arange(nblocks, dtype=jnp.int32)
    first_hit = jnp.transpose(blocks[:, :, 0:1] == block_ids, (1, 0, 2))
    second_hit = jnp.transpose(blocks[:, :, 1:2] == block_ids, (1, 0, 2))
    low_end = jnp.minimum(wedge[0], wedge[1])
    high_end = jnp.maximum(wedge[0], wedge[1])
    line_pos = jnp.arange(N, dtype=jnp.int32)
    excluded = ((line_pos >= low_end) & (line_pos < high_end)).reshape(nblocks, block_len)
    usable = ((first_hit | second_hit)[:, :, None, :, None]) & (~excluded)[None, None, None]
    first_pick = first_hit[:, :, None, :, None]
    kweight = ((jnp.abs(own_freq - half_freq).astype(jnp.float32) + 1.0) / half_freq)[
        None, None, :, None, None
    ]
    shape_five = (2, N, per_device, nblocks, block_len)

    def substitute(polar, part):
        m0 = measured[:, part, :, :, 0][:, :, :, None, :]
        m1 = measured[:, part, :, :, 1][:, :, :, None, :]
        picked = jnp.where(first_pick, m0, m1).astype(jnp.float32)
        value = jnp.where(usable, picked, polar.reshape(shape_five)) * kweight
        return value.reshape(2, N, per_device, N).astype(jnp.bfloat16)

    weighted_re = substitute(polar_re, 0)
    weighted_im = substitute(polar_im, 1)
    adj_re = (
        contract("klc,gakl->gakc", frac_cos, weighted_re)
        - contract("klc,gakl->gakc", frac_sin, weighted_im)
    ).astype(jnp.bfloat16)
    adj_im = (
        contract("klc,gakl->gakc", frac_cos, weighted_im)
        + contract("klc,gakl->gakc", frac_sin, weighted_re)
    ).astype(jnp.bfloat16)
    plan_re = (
        contract("az,gakc->gzkc", dz_cos, adj_re) - contract("az,gakc->gzkc", dz_sin, adj_im)
    ).astype(jnp.bfloat16)
    plan_im = (
        contract("az,gakc->gzkc", dz_cos, adj_im) + contract("az,gakc->gzkc", dz_sin, adj_re)
    ).astype(jnp.bfloat16)
    returned = lax.all_to_all(
        jnp.stack([plan_re, plan_im], axis=1), "slab", split_axis=2, concat_axis=3, tiled=True
    )
    spread = lax.all_to_all(returned, "line", split_axis=4, concat_axis=3, tiled=True)
    image_b = contract("ky,zkx->zxy", back_cos, spread[1, 0]) - contract(
        "ky,zkx->zxy", back_sin, spread[1, 1]
    )
    image_a = contract("kx,zky->zxy", back_cos, spread[0, 0]) - contract(
        "kx,zky->zxy", back_sin, spread[0, 1]
    )
    image_a = lax.all_to_all(image_a, "line", split_axis=1, concat_axis=2, tiled=True)
    summed = image_a + image_b
    ycoord = jnp.arange(obj_len, dtype=jnp.int32)
    inside = (ycoord[None, None, :] >= support_lo[:, :, None]) & (
        ycoord[None, None, :] < support_hi[:, :, None]
    )
    return jnp.where(inside & (summed > 0.0), summed, jnp.float32(0.0))


def solution(mesh):
    in_specs = (
        P("slab", "line", None),
        P("slab", "line"),
        P("slab", "line"),
        P(None, None, None, ("slab", "line"), None, None),
        P(),
        P(),
    )
    out_specs = P("slab", "line", None)
    return jax.shard_map(shards, mesh=mesh, in_specs=in_specs, out_specs=out_specs, check_vma=False)
```

```python
import math

import jax
import jax.numpy as jnp
from jax import lax
from jax.sharding import PartitionSpec as P

N = 512


def phase_table(left_int, right_int, period):
    product = jnp.mod(left_int * right_int, period)
    angle = product.astype(jnp.float32) * (2.0 * math.pi / period)
    factor = 1.0 / math.sqrt(N)
    return (
        (jnp.cos(angle) * factor).astype(jnp.bfloat16),
        (jnp.sin(angle) * factor).astype(jnp.bfloat16),
    )


def contract(form, left_op, right_op):
    return jnp.einsum(form, left_op, right_op, preferred_element_type=jnp.float32)


def shards(estimate, support_lo, support_hi, measured, blocks, wedge):
    slab_count = lax.axis_size("slab")
    line_count = lax.axis_size("line")
    slab_index = lax.axis_index("slab")
    line_index = lax.axis_index("line")
    plane_rows, row_count, obj_len = estimate.shape
    half_freq = N // 2
    device_count = slab_count * line_count
    per_device = N // device_count
    cell_coord = jnp.arange(obj_len, dtype=jnp.int32) - obj_len // 2
    own_freq = (slab_index * line_count + line_index) * per_device + jnp.arange(
        per_device, dtype=jnp.int32
    )
    all_freq = jnp.arange(N, dtype=jnp.int32) - half_freq
    tables = phase_table(all_freq[:, None], cell_coord[None, :], N) + phase_table(
        (2 * (own_freq - half_freq))[:, None, None] * all_freq[None, :, None],
        cell_coord[None, None, :],
        N * N,
    )
    dft_cos, dft_sin, frac_cos, frac_sin = lax.optimization_barrier(tables)

    cells = estimate.astype(jnp.bfloat16)
    planes = lax.all_to_all(cells, "line", split_axis=0, concat_axis=1, tiled=True)
    real_a = contract("kx,zxy->kzy", dft_cos, planes)
    imag_a = -contract("kx,zxy->kzy", dft_sin, planes)
    real_b = contract("ky,zxy->kzx", dft_cos, planes)
    imag_b = -contract("ky,zxy->kzx", dft_sin, planes)
    spectrum = jnp.stack([jnp.stack([real_a, imag_a]), jnp.stack([real_b, imag_b])]).astype(
        jnp.bfloat16
    )
    gathered = lax.all_to_all(
        spectrum, ("slab", "line"), split_axis=2, concat_axis=3, tiled=True
    )
    pen_re = (
        contract("az,gkzc->gkac", dft_cos, gathered[:, 0])
        + contract("az,gkzc->gkac", dft_sin, gathered[:, 1])
    ).astype(jnp.bfloat16)
    pen_im = (
        contract("az,gkzc->gkac", dft_cos, gathered[:, 1])
        - contract("az,gkzc->gkac", dft_sin, gathered[:, 0])
    ).astype(jnp.bfloat16)
    polar_re = contract("klc,gkac->gkal", frac_cos, pen_re) + contract(
        "klc,gkac->gkal", frac_sin, pen_im
    )
    polar_im = contract("klc,gkac->gkal", frac_cos, pen_im) - contract(
        "klc,gkac->gkal", frac_sin, pen_re
    )
    block_len = measured.shape[-1]
    nblocks = N // block_len
    low_end = jnp.minimum(wedge[0], wedge[1])
    high_end = jnp.maximum(wedge[0], wedge[1])
    line_pos = jnp.arange(N, dtype=jnp.int32)
    excluded = ((line_pos >= low_end) & (line_pos < high_end)).reshape(nblocks, block_len)
    kweight = (jnp.abs(own_freq - half_freq).astype(jnp.float32) + 1.0) / half_freq
    first_of = jnp.transpose(blocks[:, :, 0])[:, None, :, None]
    second_of = jnp.transpose(blocks[:, :, 1])[:, None, :, None]

    def substitute(polar, part):
        m0 = jnp.transpose(measured[:, part, :, :, 0, :], (0, 2, 1, 3))
        m1 = jnp.transpose(measured[:, part, :, :, 1, :], (0, 2, 1, 3))
        chunks = []
        for nb in range(nblocks):
            hit0 = first_of == nb
            hit1 = second_of == nb
            use = (hit0 | hit1) & (~excluded[nb])[None, None, None, :]
            picked = jnp.where(hit0, m0, m1).astype(jnp.float32)
            chunks.append(
                jnp.where(use, picked, polar[..., nb * block_len : (nb + 1) * block_len])
            )
        value = jnp.concatenate(chunks, axis=-1) * kweight[None, :, None, None]
        return value.astype(jnp.bfloat16)

    weighted_re = substitute(polar_re, 0)
    weighted_im = substitute(polar_im, 1)
    adj_re = (
        contract("klc,gkal->gkac", frac_cos, weighted_re)
        - contract("klc,gkal->gkac", frac_sin, weighted_im)
    ).astype(jnp.bfloat16)
    adj_im = (
        contract("klc,gkal->gkac", frac_cos, weighted_im)
        + contract("klc,gkal->gkac", frac_sin, weighted_re)
    ).astype(jnp.bfloat16)
    plan_re = (
        contract("az,gkac->gkzc", dft_cos, adj_re) - contract("az,gkac->gkzc", dft_sin, adj_im)
    ).astype(jnp.bfloat16)
    plan_im = (
        contract("az,gkac->gkzc", dft_cos, adj_im) + contract("az,gkac->gkzc", dft_sin, adj_re)
    ).astype(jnp.bfloat16)
    returned = lax.all_to_all(
        jnp.stack([plan_re, plan_im], axis=1),
        ("slab", "line"),
        split_axis=3,
        concat_axis=2,
        tiled=True,
    )
    image = (
        contract("kx,kzy->zxy", dft_cos, returned[0, 0])
        - contract("kx,kzy->zxy", dft_sin, returned[0, 1])
        + contract("ky,kzx->zxy", dft_cos, returned[1, 0])
        - contract("ky,kzx->zxy", dft_sin, returned[1, 1])
    )
    summed = lax.all_to_all(image, "line", split_axis=1, concat_axis=0, tiled=True)
    ycoord = jnp.arange(obj_len, dtype=jnp.int32)
    inside = (ycoord[None, None, :] >= support_lo[:, :, None]) & (
        ycoord[None, None, :] < support_hi[:, :, None]
    )
    return jnp.where(inside & (summed > 0.0), summed, jnp.float32(0.0))


def solution(mesh):
    in_specs = (
        P("slab", "line", None),
        P("slab", "line"),
        P("slab", "line"),
        P(None, None, None, ("slab", "line"), None, None),
        P(),
        P(),
    )
    out_specs = P("slab", "line", None)
    return jax.shard_map(shards, mesh=mesh, in_specs=in_specs, out_specs=out_specs, check_vma=False)
```

```python
import math

import jax
import jax.numpy as jnp
from jax import lax
from jax.sharding import PartitionSpec as P

N = 512


def phase_table(left_int, right_int, period):
    product = jnp.mod(left_int * right_int, period)
    angle = product.astype(jnp.float32) * (2.0 * math.pi / period)
    factor = 1.0 / math.sqrt(N)
    return (
        (jnp.cos(angle) * factor).astype(jnp.bfloat16),
        (jnp.sin(angle) * factor).astype(jnp.bfloat16),
    )


def contract(form, left_op, right_op):
    return jnp.einsum(form, left_op, right_op, preferred_element_type=jnp.float32)


def shards(estimate, support_lo, support_hi, measured, blocks, wedge):
    slab_count = lax.axis_size("slab")
    line_count = lax.axis_size("line")
    slab_index = lax.axis_index("slab")
    line_index = lax.axis_index("line")
    plane_rows, row_count, obj_len = estimate.shape
    half_freq = N // 2
    device_count = slab_count * line_count
    per_device = N // device_count
    cell_coord = jnp.arange(obj_len, dtype=jnp.int32) - obj_len // 2
    own_freq = (slab_index * line_count + line_index) * per_device + jnp.arange(
        per_device, dtype=jnp.int32
    )
    all_freq = jnp.arange(N, dtype=jnp.int32) - half_freq
    tables = phase_table(all_freq[:, None], cell_coord[None, :], N) + phase_table(
        (2 * (own_freq - half_freq))[:, None, None] * all_freq[None, :, None],
        cell_coord[None, None, :],
        N * N,
    )
    dft_cos, dft_sin, frac_cos, frac_sin = lax.optimization_barrier(tables)

    cells = estimate.astype(jnp.bfloat16)
    planes = lax.all_to_all(cells, "line", split_axis=0, concat_axis=1, tiled=True)
    forward_forms = ("kx,zxy->kzy", "ky,zxy->kzx")
    backward_forms = ("kx,kzy->zxy", "ky,kzx->zxy")
    block_len = measured.shape[-1]
    nblocks = N // block_len
    low_end = jnp.minimum(wedge[0], wedge[1])
    high_end = jnp.maximum(wedge[0], wedge[1])
    line_pos = jnp.arange(N, dtype=jnp.int32)
    excluded = ((line_pos >= low_end) & (line_pos < high_end)).reshape(nblocks, block_len)
    kweight = (jnp.abs(own_freq - half_freq).astype(jnp.float32) + 1.0) / half_freq
    measured_t = jnp.transpose(measured, (3, 0, 1, 4, 2, 5))

    def substitute(polar, group, part):
        m0 = measured_t[:, group, part, 0]
        m1 = measured_t[:, group, part, 1]
        first_of = blocks[:, group, 0][None, :, None]
        second_of = blocks[:, group, 1][None, :, None]
        chunks = []
        for nb in range(nblocks):
            hit0 = first_of == nb
            hit1 = second_of == nb
            use = (hit0 | hit1) & (~excluded[nb])[None, None, :]
            picked = jnp.where(hit0, m0, m1).astype(jnp.float32)
            chunks.append(
                jnp.where(use, picked, polar[..., nb * block_len : (nb + 1) * block_len])
            )
        value = jnp.concatenate(chunks, axis=-1) * kweight[:, None, None]
        return value.astype(jnp.bfloat16)

    image = None
    for group in range(2):
        real = contract(forward_forms[group], dft_cos, planes)
        imag = -contract(forward_forms[group], dft_sin, planes)
        spectrum = jnp.stack([real, imag]).astype(jnp.bfloat16)
        gathered = lax.all_to_all(
            spectrum, ("slab", "line"), split_axis=1, concat_axis=2, tiled=True
        )
        pen_re = (
            contract("az,kzc->kac", dft_cos, gathered[0])
            + contract("az,kzc->kac", dft_sin, gathered[1])
        ).astype(jnp.bfloat16)
        pen_im = (
            contract("az,kzc->kac", dft_cos, gathered[1])
            - contract("az,kzc->kac", dft_sin, gathered[0])
        ).astype(jnp.bfloat16)
        polar_re = contract("klc,kac->kal", frac_cos, pen_re) + contract(
            "klc,kac->kal", frac_sin, pen_im
        )
        polar_im = contract("klc,kac->kal", frac_cos, pen_im) - contract(
            "klc,kac->kal", frac_sin, pen_re
        )
        weighted_re = substitute(polar_re, group, 0)
        weighted_im = substitute(polar_im, group, 1)
        adj_re = (
            contract("klc,kal->kac", frac_cos, weighted_re)
            - contract("klc,kal->kac", frac_sin, weighted_im)
        ).astype(jnp.bfloat16)
        adj_im = (
            contract("klc,kal->kac", frac_cos, weighted_im)
            + contract("klc,kal->kac", frac_sin, weighted_re)
        ).astype(jnp.bfloat16)
        plan_re = (
            contract("az,kac->kzc", dft_cos, adj_re) - contract("az,kac->kzc", dft_sin, adj_im)
        ).astype(jnp.bfloat16)
        plan_im = (
            contract("az,kac->kzc", dft_cos, adj_im) + contract("az,kac->kzc", dft_sin, adj_re)
        ).astype(jnp.bfloat16)
        returned = lax.all_to_all(
            jnp.stack([plan_re, plan_im]),
            ("slab", "line"),
            split_axis=2,
            concat_axis=1,
            tiled=True,
        )
        part_image = contract(backward_forms[group], dft_cos, returned[0]) - contract(
            backward_forms[group], dft_sin, returned[1]
        )
        image = part_image if image is None else image + part_image
    summed = lax.all_to_all(image, "line", split_axis=1, concat_axis=0, tiled=True)
    ycoord = jnp.arange(obj_len, dtype=jnp.int32)
    inside = (ycoord[None, None, :] >= support_lo[:, :, None]) & (
        ycoord[None, None, :] < support_hi[:, :, None]
    )
    return jnp.where(inside & (summed > 0.0), summed, jnp.float32(0.0))


def solution(mesh):
    in_specs = (
        P("slab", "line", None),
        P("slab", "line"),
        P("slab", "line"),
        P(None, None, None, ("slab", "line"), None, None),
        P(),
        P(),
    )
    out_specs = P("slab", "line", None)
    return jax.shard_map(shards, mesh=mesh, in_specs=in_specs, out_specs=out_specs, check_vma=False)
```

```python
import math

import jax
import jax.numpy as jnp
from jax import lax
from jax.sharding import PartitionSpec as P

N = 512


def phase_table(left_int, right_int, period):
    product = jnp.mod(left_int * right_int, period)
    angle = product.astype(jnp.float32) * (2.0 * math.pi / period)
    factor = 1.0 / math.sqrt(N)
    return (
        (jnp.cos(angle) * factor).astype(jnp.bfloat16),
        (jnp.sin(angle) * factor).astype(jnp.bfloat16),
    )


def contract(form, left_op, right_op):
    return jnp.einsum(form, left_op, right_op, preferred_element_type=jnp.float32)


def shards(estimate, support_lo, support_hi, measured, blocks, wedge):
    slab_count = lax.axis_size("slab")
    line_count = lax.axis_size("line")
    slab_index = lax.axis_index("slab")
    line_index = lax.axis_index("line")
    plane_rows, row_count, obj_len = estimate.shape
    half_freq = N // 2
    device_count = slab_count * line_count
    per_device = N // device_count
    cell_coord = jnp.arange(obj_len, dtype=jnp.int32) - obj_len // 2
    own_freq = (slab_index * line_count + line_index) * per_device + jnp.arange(
        per_device, dtype=jnp.int32
    )
    all_freq = jnp.arange(N, dtype=jnp.int32) - half_freq
    tables = phase_table(all_freq[:, None], cell_coord[None, :], N) + phase_table(
        (2 * (own_freq - half_freq))[:, None, None] * all_freq[None, :, None],
        cell_coord[None, None, :],
        N * N,
    )
    dft_cos, dft_sin, frac_cos, frac_sin = lax.optimization_barrier(tables)

    cells = estimate.astype(jnp.bfloat16)
    planes = lax.all_to_all(cells, "line", split_axis=0, concat_axis=1, tiled=True)
    block_len = measured.shape[-1]
    nblocks = N // block_len
    low_end = jnp.minimum(wedge[0], wedge[1])
    high_end = jnp.maximum(wedge[0], wedge[1])
    line_pos = jnp.arange(N, dtype=jnp.int32)
    excluded = ((line_pos >= low_end) & (line_pos < high_end)).reshape(nblocks, block_len)
    kweight = (jnp.abs(own_freq - half_freq).astype(jnp.float32) + 1.0) / half_freq
    measured_t = jnp.transpose(measured, (3, 0, 1, 4, 2, 5))

    def substitute(polar, group, part):
        m0 = measured_t[:, group, part, 0]
        m1 = measured_t[:, group, part, 1]
        first_of = blocks[:, group, 0][None, :, None]
        second_of = blocks[:, group, 1][None, :, None]
        chunks = []
        for nb in range(nblocks):
            hit0 = first_of == nb
            hit1 = second_of == nb
            use = (hit0 | hit1) & (~excluded[nb])[None, None, :]
            picked = jnp.where(hit0, m0, m1).astype(jnp.float32)
            chunks.append(
                jnp.where(use, picked, polar[..., nb * block_len : (nb + 1) * block_len])
            )
        value = jnp.concatenate(chunks, axis=-1) * kweight[:, None, None]
        return value.astype(jnp.bfloat16)

    slab_planes = plane_rows

    def spectrum_of(group):
        if group == 0:
            real = contract("kx,zxy->kzy", dft_cos, planes)
            imag = -contract("kx,zxy->kzy", dft_sin, planes)
            spectrum = jnp.stack([real, imag]).astype(jnp.bfloat16)
            return lax.all_to_all(
                spectrum, ("slab", "line"), split_axis=1, concat_axis=2, tiled=True
            )
        rows = cells.reshape(plane_rows * row_count, obj_len)
        real = contract("ky,ny->kn", dft_cos, rows)
        imag = -contract("ky,ny->kn", dft_sin, rows)
        spectrum = jnp.stack([real, imag]).astype(jnp.bfloat16)[:, :, None, :]
        moved = lax.all_to_all(
            spectrum, ("slab", "line"), split_axis=1, concat_axis=2, tiled=True
        )
        moved = moved.reshape(2, per_device, slab_count, line_count, plane_rows, row_count)
        moved = jnp.transpose(moved, (0, 1, 2, 4, 3, 5))
        return moved.reshape(2, per_device, slab_count * plane_rows, line_count * row_count)

    def planar_of(group, gathered):
        pen_re = (
            contract("az,kzc->kac", dft_cos, gathered[0])
            + contract("az,kzc->kac", dft_sin, gathered[1])
        ).astype(jnp.bfloat16)
        pen_im = (
            contract("az,kzc->kac", dft_cos, gathered[1])
            - contract("az,kzc->kac", dft_sin, gathered[0])
        ).astype(jnp.bfloat16)
        polar_re = contract("klc,kac->kal", frac_cos, pen_re) + contract(
            "klc,kac->kal", frac_sin, pen_im
        )
        polar_im = contract("klc,kac->kal", frac_cos, pen_im) - contract(
            "klc,kac->kal", frac_sin, pen_re
        )
        weighted_re = substitute(polar_re, group, 0)
        weighted_im = substitute(polar_im, group, 1)
        adj_re = (
            contract("klc,kal->kac", frac_cos, weighted_re)
            - contract("klc,kal->kac", frac_sin, weighted_im)
        ).astype(jnp.bfloat16)
        adj_im = (
            contract("klc,kal->kac", frac_cos, weighted_im)
            + contract("klc,kal->kac", frac_sin, weighted_re)
        ).astype(jnp.bfloat16)
        plan_re = (
            contract("az,kac->kzc", dft_cos, adj_re) - contract("az,kac->kzc", dft_sin, adj_im)
        ).astype(jnp.bfloat16)
        plan_im = (
            contract("az,kac->kzc", dft_cos, adj_im) + contract("az,kac->kzc", dft_sin, adj_re)
        ).astype(jnp.bfloat16)
        return jnp.stack([plan_re, plan_im])

    gathered_a = spectrum_of(0)
    gathered_b = spectrum_of(1)
    plan_a = planar_of(0, gathered_a)
    returned_a = lax.all_to_all(plan_a, ("slab", "line"), split_axis=2, concat_axis=1, tiled=True)
    image_a = contract("kx,kzy->zxy", dft_cos, returned_a[0]) - contract(
        "kx,kzy->zxy", dft_sin, returned_a[1]
    )
    image_a = lax.all_to_all(image_a, "line", split_axis=1, concat_axis=0, tiled=True)
    plan_b = planar_of(1, gathered_b)
    plan_b = plan_b.reshape(2, per_device, slab_count, slab_planes, line_count, row_count)
    plan_b = jnp.transpose(plan_b, (0, 1, 2, 4, 3, 5)).reshape(
        2, per_device, device_count, slab_planes * row_count
    )
    returned_b = lax.all_to_all(plan_b, ("slab", "line"), split_axis=2, concat_axis=1, tiled=True)
    image_b = contract("ky,kn->ny", dft_cos, returned_b[0, :, 0]) - contract(
        "ky,kn->ny", dft_sin, returned_b[1, :, 0]
    )
    summed = image_a + image_b.reshape(plane_rows, row_count, obj_len)
    ycoord = jnp.arange(obj_len, dtype=jnp.int32)
    inside = (ycoord[None, None, :] >= support_lo[:, :, None]) & (
        ycoord[None, None, :] < support_hi[:, :, None]
    )
    return jnp.where(inside & (summed > 0.0), summed, jnp.float32(0.0))


def solution(mesh):
    in_specs = (
        P("slab", "line", None),
        P("slab", "line"),
        P("slab", "line"),
        P(None, None, None, ("slab", "line"), None, None),
        P(),
        P(),
    )
    out_specs = P("slab", "line", None)
    return jax.shard_map(shards, mesh=mesh, in_specs=in_specs, out_specs=out_specs, check_vma=False)
```

```python
import math

import jax
import jax.numpy as jnp
from jax import lax
from jax.sharding import PartitionSpec as P

N = 512


def phase_table(left_int, right_int, period):
    product = jnp.mod(left_int * right_int, period)
    angle = product.astype(jnp.float32) * (2.0 * math.pi / period)
    factor = 1.0 / math.sqrt(N)
    return (
        (jnp.cos(angle) * factor).astype(jnp.bfloat16),
        (jnp.sin(angle) * factor).astype(jnp.bfloat16),
    )


def contract(form, left_op, right_op):
    return jnp.einsum(form, left_op, right_op, preferred_element_type=jnp.float32)


def shards(estimate, support_lo, support_hi, measured, blocks, wedge):
    slab_count = lax.axis_size("slab")
    line_count = lax.axis_size("line")
    slab_index = lax.axis_index("slab")
    line_index = lax.axis_index("line")
    plane_rows, row_count, obj_len = estimate.shape
    half_freq = N // 2
    device_count = slab_count * line_count
    per_device = N // device_count
    cell_coord = jnp.arange(obj_len, dtype=jnp.int32) - obj_len // 2
    own_freq = (slab_index * line_count + line_index) * per_device + jnp.arange(
        per_device, dtype=jnp.int32
    )
    all_freq = jnp.arange(N, dtype=jnp.int32) - half_freq
    tables = phase_table(all_freq[:, None], cell_coord[None, :], N) + phase_table(
        (2 * (own_freq - half_freq))[:, None, None] * all_freq[None, :, None],
        cell_coord[None, None, :],
        N * N,
    )
    dft_cos, dft_sin, frac_cos, frac_sin = lax.optimization_barrier(tables)

    cells = estimate.astype(jnp.bfloat16)
    planes = lax.all_to_all(cells, "line", split_axis=0, concat_axis=1, tiled=True)
    forward_forms = ("kx,zxy->kzy", "ky,zxy->kzx")
    backward_forms = ("kx,kzy->zxy", "ky,kzx->zxy")
    block_len = measured.shape[-1]
    nblocks = N // block_len
    low_end = jnp.minimum(wedge[0], wedge[1])
    high_end = jnp.maximum(wedge[0], wedge[1])
    line_pos = jnp.arange(N, dtype=jnp.int32)
    excluded = ((line_pos >= low_end) & (line_pos < high_end)).reshape(nblocks, block_len)
    kweight = (jnp.abs(own_freq - half_freq).astype(jnp.float32) + 1.0) / half_freq
    measured_t = jnp.transpose(measured, (3, 0, 1, 4, 2, 5))

    def substitute(polar, group, part):
        m0 = measured_t[:, group, part, 0]
        m1 = measured_t[:, group, part, 1]
        first_of = blocks[:, group, 0][None, :, None]
        second_of = blocks[:, group, 1][None, :, None]
        chunks = []
        for nb in range(nblocks):
            hit0 = first_of == nb
            hit1 = second_of == nb
            use = (hit0 | hit1) & (~excluded[nb])[None, None, :]
            picked = jnp.where(hit0, m0, m1).astype(jnp.float32)
            chunks.append(
                jnp.where(use, picked, polar[..., nb * block_len : (nb + 1) * block_len])
            )
        value = jnp.concatenate(chunks, axis=-1) * kweight[:, None, None]
        return value.astype(jnp.bfloat16)

    def spectrum_of(group):
        real = contract(forward_forms[group], dft_cos, planes)
        imag = -contract(forward_forms[group], dft_sin, planes)
        spectrum = jnp.stack([real, imag]).astype(jnp.bfloat16)
        return lax.all_to_all(
            spectrum, ("slab", "line"), split_axis=1, concat_axis=2, tiled=True
        )

    def planar_of(group, gathered):
        pen_re = (
            contract("az,kzc->kac", dft_cos, gathered[0])
            + contract("az,kzc->kac", dft_sin, gathered[1])
        ).astype(jnp.bfloat16)
        pen_im = (
            contract("az,kzc->kac", dft_cos, gathered[1])
            - contract("az,kzc->kac", dft_sin, gathered[0])
        ).astype(jnp.bfloat16)
        polar_re = contract("klc,kac->kal", frac_cos, pen_re) + contract(
            "klc,kac->kal", frac_sin, pen_im
        )
        polar_im = contract("klc,kac->kal", frac_cos, pen_im) - contract(
            "klc,kac->kal", frac_sin, pen_re
        )
        weighted_re = substitute(polar_re, group, 0)
        weighted_im = substitute(polar_im, group, 1)
        adj_re = (
            contract("klc,kal->kac", frac_cos, weighted_re)
            - contract("klc,kal->kac", frac_sin, weighted_im)
        ).astype(jnp.bfloat16)
        adj_im = (
            contract("klc,kal->kac", frac_cos, weighted_im)
            + contract("klc,kal->kac", frac_sin, weighted_re)
        ).astype(jnp.bfloat16)
        plan_re = (
            contract("az,kac->kzc", dft_cos, adj_re) - contract("az,kac->kzc", dft_sin, adj_im)
        ).astype(jnp.bfloat16)
        plan_im = (
            contract("az,kac->kzc", dft_cos, adj_im) + contract("az,kac->kzc", dft_sin, adj_re)
        ).astype(jnp.bfloat16)
        return jnp.stack([plan_re, plan_im])

    def returned_of(plan):
        return lax.all_to_all(plan, ("slab", "line"), split_axis=2, concat_axis=1, tiled=True)

    def image_of(group, returned):
        return contract(backward_forms[group], dft_cos, returned[0]) - contract(
            backward_forms[group], dft_sin, returned[1]
        )

    gathered_a = spectrum_of(0)
    gathered_b = spectrum_of(1)
    plan_a = planar_of(0, gathered_a)
    plan_a, gathered_b = lax.optimization_barrier((plan_a, gathered_b))
    image_a = image_of(0, returned_of(plan_a))
    plan_b = planar_of(1, gathered_b)
    image = image_a + image_of(1, returned_of(plan_b))
    image = lax.all_to_all(image, "line", split_axis=1, concat_axis=0, tiled=True)
    summed = image
    ycoord = jnp.arange(obj_len, dtype=jnp.int32)
    inside = (ycoord[None, None, :] >= support_lo[:, :, None]) & (
        ycoord[None, None, :] < support_hi[:, :, None]
    )
    return jnp.where(inside & (summed > 0.0), summed, jnp.float32(0.0))


def solution(mesh):
    in_specs = (
        P("slab", "line", None),
        P("slab", "line"),
        P("slab", "line"),
        P(None, None, None, ("slab", "line"), None, None),
        P(),
        P(),
    )
    out_specs = P("slab", "line", None)
    return jax.shard_map(shards, mesh=mesh, in_specs=in_specs, out_specs=out_specs, check_vma=False)
```

```python
import math

import jax
import jax.numpy as jnp
from jax import lax
from jax.sharding import PartitionSpec as P

N = 512


def phase_table(left_int, right_int, period):
    product = jnp.mod(left_int * right_int, period)
    angle = product.astype(jnp.float32) * (2.0 * math.pi / period)
    factor = 1.0 / math.sqrt(N)
    return (
        (jnp.cos(angle) * factor).astype(jnp.bfloat16),
        (jnp.sin(angle) * factor).astype(jnp.bfloat16),
    )


def contract(form, left_op, right_op):
    return jnp.einsum(form, left_op, right_op, preferred_element_type=jnp.float32)


def shards(estimate, support_lo, support_hi, measured, blocks, wedge):
    slab_count = lax.axis_size("slab")
    line_count = lax.axis_size("line")
    slab_index = lax.axis_index("slab")
    line_index = lax.axis_index("line")
    plane_rows, row_count, obj_len = estimate.shape
    half_freq = N // 2
    device_count = slab_count * line_count
    per_device = N // device_count
    cell_coord = jnp.arange(obj_len, dtype=jnp.int32) - obj_len // 2
    own_freq = (slab_index * line_count + line_index) * per_device + jnp.arange(
        per_device, dtype=jnp.int32
    )
    all_freq = jnp.arange(N, dtype=jnp.int32) - half_freq
    dft_cos, dft_sin = lax.optimization_barrier(
        phase_table(all_freq[:, None], cell_coord[None, :], N)
    )
    frac_rows = (2 * (own_freq - half_freq))[:, None, None] * all_freq[None, :, None]

    cells = estimate.astype(jnp.bfloat16)
    planes = lax.all_to_all(cells, "line", split_axis=0, concat_axis=1, tiled=True)
    forward_forms = ("kx,zxy->kzy", "ky,zxy->kzx")
    backward_forms = ("kx,kzy->zxy", "ky,kzx->zxy")
    block_len = measured.shape[-1]
    nblocks = N // block_len
    low_end = jnp.minimum(wedge[0], wedge[1])
    high_end = jnp.maximum(wedge[0], wedge[1])
    line_pos = jnp.arange(N, dtype=jnp.int32)
    excluded = ((line_pos >= low_end) & (line_pos < high_end)).reshape(nblocks, block_len)
    kweight = (jnp.abs(own_freq - half_freq).astype(jnp.float32) + 1.0) / half_freq
    measured_t = jnp.transpose(measured, (3, 0, 1, 4, 2, 5))

    def substitute(polar, group, part):
        m0 = measured_t[:, group, part, 0]
        m1 = measured_t[:, group, part, 1]
        first_of = blocks[:, group, 0][None, :, None]
        second_of = blocks[:, group, 1][None, :, None]
        chunks = []
        for nb in range(nblocks):
            hit0 = first_of == nb
            hit1 = second_of == nb
            use = (hit0 | hit1) & (~excluded[nb])[None, None, :]
            picked = jnp.where(hit0, m0, m1).astype(jnp.float32)
            chunks.append(
                jnp.where(use, picked, polar[..., nb * block_len : (nb + 1) * block_len])
            )
        value = jnp.concatenate(chunks, axis=-1) * kweight[:, None, None]
        return value.astype(jnp.bfloat16)

    def spectrum_of(group):
        real = contract(forward_forms[group], dft_cos, planes)
        imag = -contract(forward_forms[group], dft_sin, planes)
        return jnp.stack([real, imag]).astype(jnp.bfloat16)

    def exchange(spectrum):
        return lax.all_to_all(
            spectrum, ("slab", "line"), split_axis=1, concat_axis=2, tiled=True
        )

    def planar_of(group, gathered):
        pen_re = (
            contract("az,kzc->kac", dft_cos, gathered[0])
            + contract("az,kzc->kac", dft_sin, gathered[1])
        ).astype(jnp.bfloat16)
        pen_im = (
            contract("az,kzc->kac", dft_cos, gathered[1])
            - contract("az,kzc->kac", dft_sin, gathered[0])
        ).astype(jnp.bfloat16)
        polar_re = contract("klc,kac->kal", frac_cos, pen_re) + contract(
            "klc,kac->kal", frac_sin, pen_im
        )
        polar_im = contract("klc,kac->kal", frac_cos, pen_im) - contract(
            "klc,kac->kal", frac_sin, pen_re
        )
        weighted_re = substitute(polar_re, group, 0)
        weighted_im = substitute(polar_im, group, 1)
        adj_re = (
            contract("klc,kal->kac", frac_cos, weighted_re)
            - contract("klc,kal->kac", frac_sin, weighted_im)
        ).astype(jnp.bfloat16)
        adj_im = (
            contract("klc,kal->kac", frac_cos, weighted_im)
            + contract("klc,kal->kac", frac_sin, weighted_re)
        ).astype(jnp.bfloat16)
        plan_re = (
            contract("az,kac->kzc", dft_cos, adj_re) - contract("az,kac->kzc", dft_sin, adj_im)
        ).astype(jnp.bfloat16)
        plan_im = (
            contract("az,kac->kzc", dft_cos, adj_im) + contract("az,kac->kzc", dft_sin, adj_re)
        ).astype(jnp.bfloat16)
        return jnp.stack([plan_re, plan_im])

    def returned_of(plan):
        return lax.all_to_all(plan, ("slab", "line"), split_axis=2, concat_axis=1, tiled=True)

    def image_of(group, returned):
        return contract(backward_forms[group], dft_cos, returned[0]) - contract(
            backward_forms[group], dft_sin, returned[1]
        )

    spectrum_a = spectrum_of(0)
    spectrum_a, frac_rows = lax.optimization_barrier((spectrum_a, frac_rows))
    frac_cos, frac_sin = lax.optimization_barrier(
        phase_table(frac_rows, cell_coord[None, None, :], N * N)
    )
    gathered_a = exchange(spectrum_a)
    gathered_b = exchange(spectrum_of(1))
    plan_a = planar_of(0, gathered_a)
    plan_a, gathered_b = lax.optimization_barrier((plan_a, gathered_b))
    image_a = image_of(0, returned_of(plan_a))
    plan_b = planar_of(1, gathered_b)
    image = image_a + image_of(1, returned_of(plan_b))
    image = lax.all_to_all(image, "line", split_axis=1, concat_axis=0, tiled=True)
    summed = image
    ycoord = jnp.arange(obj_len, dtype=jnp.int32)
    inside = (ycoord[None, None, :] >= support_lo[:, :, None]) & (
        ycoord[None, None, :] < support_hi[:, :, None]
    )
    return jnp.where(inside & (summed > 0.0), summed, jnp.float32(0.0))


def solution(mesh):
    in_specs = (
        P("slab", "line", None),
        P("slab", "line"),
        P("slab", "line"),
        P(None, None, None, ("slab", "line"), None, None),
        P(),
        P(),
    )
    out_specs = P("slab", "line", None)
    return jax.shard_map(shards, mesh=mesh, in_specs=in_specs, out_specs=out_specs, check_vma=False)
```

```python
import math

import jax
import jax.numpy as jnp
from jax import lax
from jax.sharding import PartitionSpec as P

N = 512


def phase_table(left_int, right_int, period):
    product = jnp.mod(left_int * right_int, period)
    angle = product.astype(jnp.float32) * (2.0 * math.pi / period)
    factor = 1.0 / math.sqrt(N)
    return (
        (jnp.cos(angle) * factor).astype(jnp.bfloat16),
        (jnp.sin(angle) * factor).astype(jnp.bfloat16),
    )


def contract(form, left_op, right_op):
    return jnp.einsum(form, left_op, right_op, preferred_element_type=jnp.float32)


def shards(estimate, support_lo, support_hi, measured, blocks, wedge):
    slab_count = lax.axis_size("slab")
    line_count = lax.axis_size("line")
    slab_index = lax.axis_index("slab")
    line_index = lax.axis_index("line")
    plane_rows, row_count, obj_len = estimate.shape
    half_freq = N // 2
    device_count = slab_count * line_count
    per_device = N // device_count
    cell_coord = jnp.arange(obj_len, dtype=jnp.int32) - obj_len // 2
    own_freq = (slab_index * line_count + line_index) * per_device + jnp.arange(
        per_device, dtype=jnp.int32
    )
    all_freq = jnp.arange(N, dtype=jnp.int32) - half_freq
    dft_cos, dft_sin = lax.optimization_barrier(
        phase_table(all_freq[:, None], cell_coord[None, :], N)
    )
    frac_rows = (2 * (own_freq - half_freq))[:, None, None] * all_freq[None, :, None]

    cells = estimate.astype(jnp.bfloat16)
    planes = lax.all_to_all(cells, "line", split_axis=0, concat_axis=1, tiled=True)
    forward_forms = ("kx,zxy->kzy", "ky,zxy->kzx")
    backward_forms = ("kx,kzy->zxy", "ky,kzx->zxy")
    block_len = measured.shape[-1]
    nblocks = N // block_len
    low_end = jnp.minimum(wedge[0], wedge[1])
    high_end = jnp.maximum(wedge[0], wedge[1])
    line_pos = jnp.arange(N, dtype=jnp.int32)
    excluded = ((line_pos >= low_end) & (line_pos < high_end)).reshape(nblocks, block_len)
    kweight = (jnp.abs(own_freq - half_freq).astype(jnp.float32) + 1.0) / half_freq
    measured_t = jnp.transpose(measured, (3, 0, 1, 4, 2, 5))

    def substitute(polar, group, part):
        m0 = measured_t[:, group, part, 0]
        m1 = measured_t[:, group, part, 1]
        first_of = blocks[:, group, 0][None, :, None]
        second_of = blocks[:, group, 1][None, :, None]
        chunks = []
        for nb in range(nblocks):
            hit0 = first_of == nb
            hit1 = second_of == nb
            use = (hit0 | hit1) & (~excluded[nb])[None, None, :]
            picked = jnp.where(hit0, m0, m1).astype(jnp.float32)
            chunks.append(
                jnp.where(use, picked, polar[..., nb * block_len : (nb + 1) * block_len])
            )
        value = jnp.concatenate(chunks, axis=-1) * kweight[:, None, None]
        return value.astype(jnp.bfloat16)

    def spectrum_of(group):
        real = contract(forward_forms[group], dft_cos, planes)
        imag = -contract(forward_forms[group], dft_sin, planes)
        return jnp.stack([real, imag]).astype(jnp.bfloat16)

    def exchange(spectrum):
        return lax.all_to_all(
            spectrum, ("slab", "line"), split_axis=1, concat_axis=2, tiled=True
        )

    def planar_of(group, gathered):
        pen_re = (
            contract("az,kzc->kac", dft_cos, gathered[0])
            + contract("az,kzc->kac", dft_sin, gathered[1])
        ).astype(jnp.bfloat16)
        pen_im = (
            contract("az,kzc->kac", dft_cos, gathered[1])
            - contract("az,kzc->kac", dft_sin, gathered[0])
        ).astype(jnp.bfloat16)
        polar_re = contract("klc,kac->kal", frac_cos, pen_re) + contract(
            "klc,kac->kal", frac_sin, pen_im
        )
        polar_im = contract("klc,kac->kal", frac_cos, pen_im) - contract(
            "klc,kac->kal", frac_sin, pen_re
        )
        weighted_re = substitute(polar_re, group, 0)
        weighted_im = substitute(polar_im, group, 1)
        adj_re = (
            contract("klc,kal->kac", frac_cos, weighted_re)
            - contract("klc,kal->kac", frac_sin, weighted_im)
        ).astype(jnp.bfloat16)
        adj_im = (
            contract("klc,kal->kac", frac_cos, weighted_im)
            + contract("klc,kal->kac", frac_sin, weighted_re)
        ).astype(jnp.bfloat16)
        plan_re = (
            contract("az,kac->kzc", dft_cos, adj_re) - contract("az,kac->kzc", dft_sin, adj_im)
        ).astype(jnp.bfloat16)
        plan_im = (
            contract("az,kac->kzc", dft_cos, adj_im) + contract("az,kac->kzc", dft_sin, adj_re)
        ).astype(jnp.bfloat16)
        return jnp.stack([plan_re, plan_im])

    def returned_of(plan):
        return lax.all_to_all(plan, ("slab", "line"), split_axis=2, concat_axis=1, tiled=True)

    def image_of(group, returned):
        return contract(backward_forms[group], dft_cos, returned[0]) - contract(
            backward_forms[group], dft_sin, returned[1]
        )

    spectrum_a = spectrum_of(0)
    spectrum_a, frac_rows = lax.optimization_barrier((spectrum_a, frac_rows))
    frac_cos, frac_sin = lax.optimization_barrier(
        phase_table(frac_rows, cell_coord[None, None, :], N * N)
    )
    gathered_a = exchange(spectrum_a)
    gathered_b = exchange(spectrum_of(1))
    plan_a = planar_of(0, gathered_a)
    plan_a, gathered_b = lax.optimization_barrier((plan_a, gathered_b))
    image_a = image_of(0, returned_of(plan_a))
    plan_b = planar_of(1, gathered_b)
    image = image_a + image_of(1, returned_of(plan_b))
    image = lax.all_to_all(
        image.astype(jnp.bfloat16), "line", split_axis=1, concat_axis=0, tiled=True
    ).astype(jnp.float32)
    summed = image
    ycoord = jnp.arange(obj_len, dtype=jnp.int32)
    inside = (ycoord[None, None, :] >= support_lo[:, :, None]) & (
        ycoord[None, None, :] < support_hi[:, :, None]
    )
    return jnp.where(inside & (summed > 0.0), summed, jnp.float32(0.0))


def solution(mesh):
    in_specs = (
        P("slab", "line", None),
        P("slab", "line"),
        P("slab", "line"),
        P(None, None, None, ("slab", "line"), None, None),
        P(),
        P(),
    )
    out_specs = P("slab", "line", None)
    return jax.shard_map(shards, mesh=mesh, in_specs=in_specs, out_specs=out_specs, check_vma=False)
```

```python
import math

import jax
import jax.numpy as jnp
from jax import lax
from jax.sharding import PartitionSpec as P

N = 512


def phase_table(left_int, right_int, period):
    product = jnp.mod(left_int * right_int, period)
    angle = product.astype(jnp.float32) * (2.0 * math.pi / period)
    factor = 1.0 / math.sqrt(N)
    return (
        (jnp.cos(angle) * factor).astype(jnp.bfloat16),
        (jnp.sin(angle) * factor).astype(jnp.bfloat16),
    )


def contract(form, left_op, right_op):
    return jnp.einsum(form, left_op, right_op, preferred_element_type=jnp.float32)


def shards(estimate, support_lo, support_hi, measured, blocks, wedge):
    slab_count = lax.axis_size("slab")
    line_count = lax.axis_size("line")
    slab_index = lax.axis_index("slab")
    line_index = lax.axis_index("line")
    plane_rows, row_count, obj_len = estimate.shape
    half_freq = N // 2
    device_count = slab_count * line_count
    per_device = N // device_count
    cell_coord = jnp.arange(obj_len, dtype=jnp.int32) - obj_len // 2
    own_freq = (slab_index * line_count + line_index) * per_device + jnp.arange(
        per_device, dtype=jnp.int32
    )
    all_freq = jnp.arange(N, dtype=jnp.int32) - half_freq
    dft_cos, dft_sin = lax.optimization_barrier(
        phase_table(all_freq[:, None], cell_coord[None, :], N)
    )
    frac_rows = (2 * (own_freq - half_freq))[:, None, None] * all_freq[None, :, None]

    cells = estimate.astype(jnp.bfloat16)
    planes = lax.all_to_all(cells, "line", split_axis=0, concat_axis=1, tiled=True)
    forward_forms = ("kx,zxy->kzy", "ky,zxy->kzx")
    backward_forms = ("kx,kzy->zxy", "ky,kzx->zxy")
    block_len = measured.shape[-1]
    nblocks = N // block_len
    low_end = jnp.minimum(wedge[0], wedge[1])
    high_end = jnp.maximum(wedge[0], wedge[1])
    line_pos = jnp.arange(N, dtype=jnp.int32)
    excluded = ((line_pos >= low_end) & (line_pos < high_end)).reshape(nblocks, block_len)
    kweight = (jnp.abs(own_freq - half_freq).astype(jnp.float32) + 1.0) / half_freq
    measured_t = jnp.transpose(measured, (3, 0, 1, 4, 2, 5))
    planes, measured_t = lax.optimization_barrier((planes, measured_t))

    def substitute(polar, group, part):
        m0 = measured_t[:, group, part, 0]
        m1 = measured_t[:, group, part, 1]
        first_of = blocks[:, group, 0][None, :, None]
        second_of = blocks[:, group, 1][None, :, None]
        chunks = []
        for nb in range(nblocks):
            hit0 = first_of == nb
            hit1 = second_of == nb
            use = (hit0 | hit1) & (~excluded[nb])[None, None, :]
            picked = jnp.where(hit0, m0, m1).astype(jnp.float32)
            chunks.append(
                jnp.where(use, picked, polar[..., nb * block_len : (nb + 1) * block_len])
            )
        value = jnp.concatenate(chunks, axis=-1) * kweight[:, None, None]
        return value.astype(jnp.bfloat16)

    def spectrum_of(group):
        real = contract(forward_forms[group], dft_cos, planes)
        imag = -contract(forward_forms[group], dft_sin, planes)
        return jnp.stack([real, imag]).astype(jnp.bfloat16)

    def exchange(spectrum):
        return lax.all_to_all(
            spectrum, ("slab", "line"), split_axis=1, concat_axis=2, tiled=True
        )

    def planar_of(group, gathered):
        pen_re = (
            contract("az,kzc->kac", dft_cos, gathered[0])
            + contract("az,kzc->kac", dft_sin, gathered[1])
        ).astype(jnp.bfloat16)
        pen_im = (
            contract("az,kzc->kac", dft_cos, gathered[1])
            - contract("az,kzc->kac", dft_sin, gathered[0])
        ).astype(jnp.bfloat16)
        polar_re = contract("klc,kac->kal", frac_cos, pen_re) + contract(
            "klc,kac->kal", frac_sin, pen_im
        )
        polar_im = contract("klc,kac->kal", frac_cos, pen_im) - contract(
            "klc,kac->kal", frac_sin, pen_re
        )
        weighted_re = substitute(polar_re, group, 0)
        weighted_im = substitute(polar_im, group, 1)
        adj_re = (
            contract("klc,kal->kac", frac_cos, weighted_re)
            - contract("klc,kal->kac", frac_sin, weighted_im)
        ).astype(jnp.bfloat16)
        adj_im = (
            contract("klc,kal->kac", frac_cos, weighted_im)
            + contract("klc,kal->kac", frac_sin, weighted_re)
        ).astype(jnp.bfloat16)
        plan_re = (
            contract("az,kac->kzc", dft_cos, adj_re) - contract("az,kac->kzc", dft_sin, adj_im)
        ).astype(jnp.bfloat16)
        plan_im = (
            contract("az,kac->kzc", dft_cos, adj_im) + contract("az,kac->kzc", dft_sin, adj_re)
        ).astype(jnp.bfloat16)
        return jnp.stack([plan_re, plan_im])

    def returned_of(plan):
        return lax.all_to_all(plan, ("slab", "line"), split_axis=2, concat_axis=1, tiled=True)

    def image_of(group, returned):
        return contract(backward_forms[group], dft_cos, returned[0]) - contract(
            backward_forms[group], dft_sin, returned[1]
        )

    spectrum_a = spectrum_of(0)
    spectrum_a, frac_rows = lax.optimization_barrier((spectrum_a, frac_rows))
    frac_cos, frac_sin = lax.optimization_barrier(
        phase_table(frac_rows, cell_coord[None, None, :], N * N)
    )
    gathered_a = exchange(spectrum_a)
    gathered_b = exchange(spectrum_of(1))
    plan_a = planar_of(0, gathered_a)
    plan_a, gathered_b = lax.optimization_barrier((plan_a, gathered_b))
    image_a = image_of(0, returned_of(plan_a))
    plan_b = planar_of(1, gathered_b)
    image = image_a + image_of(1, returned_of(plan_b))
    image = lax.all_to_all(
        image.astype(jnp.bfloat16), "line", split_axis=1, concat_axis=0, tiled=True
    ).astype(jnp.float32)
    summed = image
    ycoord = jnp.arange(obj_len, dtype=jnp.int32)
    inside = (ycoord[None, None, :] >= support_lo[:, :, None]) & (
        ycoord[None, None, :] < support_hi[:, :, None]
    )
    return jnp.where(inside & (summed > 0.0), summed, jnp.float32(0.0))


def solution(mesh):
    in_specs = (
        P("slab", "line", None),
        P("slab", "line"),
        P("slab", "line"),
        P(None, None, None, ("slab", "line"), None, None),
        P(),
        P(),
    )
    out_specs = P("slab", "line", None)
    return jax.shard_map(shards, mesh=mesh, in_specs=in_specs, out_specs=out_specs, check_vma=False)
```

```python
import math

import jax
import jax.numpy as jnp
from jax import lax
from jax.sharding import PartitionSpec as P

N = 512


def phase_table(left_int, right_int, period):
    product = jnp.mod(left_int * right_int, period)
    angle = product.astype(jnp.float32) * (2.0 * math.pi / period)
    factor = 1.0 / math.sqrt(N)
    return (
        (jnp.cos(angle) * factor).astype(jnp.bfloat16),
        (jnp.sin(angle) * factor).astype(jnp.bfloat16),
    )


def contract(form, left_op, right_op):
    return jnp.einsum(form, left_op, right_op, preferred_element_type=jnp.float32)


def shards(estimate, support_lo, support_hi, measured, blocks, wedge):
    slab_count = lax.axis_size("slab")
    line_count = lax.axis_size("line")
    slab_index = lax.axis_index("slab")
    line_index = lax.axis_index("line")
    plane_rows, row_count, obj_len = estimate.shape
    half_freq = N // 2
    device_count = slab_count * line_count
    per_device = N // device_count
    cell_coord = jnp.arange(obj_len, dtype=jnp.int32) - obj_len // 2
    own_freq = (slab_index * line_count + line_index) * per_device + jnp.arange(
        per_device, dtype=jnp.int32
    )
    all_freq = jnp.arange(N, dtype=jnp.int32) - half_freq
    dft_cos, dft_sin = lax.optimization_barrier(
        phase_table(all_freq[:, None], cell_coord[None, :], N)
    )
    frac_rows = (2 * (own_freq - half_freq))[:, None, None] * all_freq[None, :, None]

    cells = estimate.astype(jnp.bfloat16)
    planes = lax.all_to_all(cells, "line", split_axis=0, concat_axis=1, tiled=True)
    forward_forms = ("kx,zxy->kzy", "ky,zxy->kzx")
    backward_forms = ("kx,kzy->zxy", "ky,kzx->zxy")
    block_len = measured.shape[-1]
    nblocks = N // block_len
    low_end = jnp.minimum(wedge[0], wedge[1])
    high_end = jnp.maximum(wedge[0], wedge[1])
    line_pos = jnp.arange(N, dtype=jnp.int32)
    excluded = ((line_pos >= low_end) & (line_pos < high_end)).reshape(nblocks, block_len)
    kweight = (jnp.abs(own_freq - half_freq).astype(jnp.float32) + 1.0) / half_freq
    measured_t = jnp.transpose(measured, (3, 0, 1, 4, 2, 5))

    def substitute(polar, group, part):
        m0 = measured_t[:, group, part, 0]
        m1 = measured_t[:, group, part, 1]
        first_of = blocks[:, group, 0][None, :, None]
        second_of = blocks[:, group, 1][None, :, None]
        chunks = []
        for nb in range(nblocks):
            hit0 = first_of == nb
            hit1 = second_of == nb
            use = (hit0 | hit1) & (~excluded[nb])[None, None, :]
            picked = jnp.where(hit0, m0, m1).astype(jnp.float32)
            chunks.append(
                jnp.where(use, picked, polar[..., nb * block_len : (nb + 1) * block_len])
            )
        value = jnp.concatenate(chunks, axis=-1) * kweight[:, None, None]
        return value.astype(jnp.bfloat16)

    def spectrum_of(group):
        real = contract(forward_forms[group], dft_cos, planes)
        imag = -contract(forward_forms[group], dft_sin, planes)
        return jnp.stack([real, imag]).astype(jnp.bfloat16)

    def exchange(spectrum):
        return lax.all_to_all(
            spectrum, ("slab", "line"), split_axis=1, concat_axis=2, tiled=True
        )

    def planar_of(group, gathered):
        pen_re = (
            contract("az,kzc->kac", dft_cos, gathered[0])
            + contract("az,kzc->kac", dft_sin, gathered[1])
        ).astype(jnp.bfloat16)
        pen_im = (
            contract("az,kzc->kac", dft_cos, gathered[1])
            - contract("az,kzc->kac", dft_sin, gathered[0])
        ).astype(jnp.bfloat16)
        polar_re = contract("klc,kac->kal", frac_cos, pen_re) + contract(
            "klc,kac->kal", frac_sin, pen_im
        )
        polar_im = contract("klc,kac->kal", frac_cos, pen_im) - contract(
            "klc,kac->kal", frac_sin, pen_re
        )
        weighted_re = substitute(polar_re, group, 0)
        weighted_im = substitute(polar_im, group, 1)
        adj_re = (
            contract("klc,kal->kac", frac_cos, weighted_re)
            - contract("klc,kal->kac", frac_sin, weighted_im)
        ).astype(jnp.bfloat16)
        adj_im = (
            contract("klc,kal->kac", frac_cos, weighted_im)
            + contract("klc,kal->kac", frac_sin, weighted_re)
        ).astype(jnp.bfloat16)
        plan_re = (
            contract("az,kac->kzc", dft_cos, adj_re) - contract("az,kac->kzc", dft_sin, adj_im)
        ).astype(jnp.bfloat16)
        plan_im = (
            contract("az,kac->kzc", dft_cos, adj_im) + contract("az,kac->kzc", dft_sin, adj_re)
        ).astype(jnp.bfloat16)
        return jnp.stack([plan_re, plan_im])

    def returned_of(plan):
        return lax.all_to_all(plan, ("slab", "line"), split_axis=2, concat_axis=1, tiled=True)

    def image_of(group, returned):
        return contract(backward_forms[group], dft_cos, returned[0]) - contract(
            backward_forms[group], dft_sin, returned[1]
        )

    spectra = jnp.stack([spectrum_of(0), spectrum_of(1)])
    spectra, frac_rows = lax.optimization_barrier((spectra, frac_rows))
    frac_cos, frac_sin = lax.optimization_barrier(
        phase_table(frac_rows, cell_coord[None, None, :], N * N)
    )
    gathered = lax.all_to_all(spectra, ("slab", "line"), split_axis=2, concat_axis=3, tiled=True)
    gathered_a, gathered_b = gathered[0], gathered[1]
    plan_a = planar_of(0, gathered_a)
    plan_a, gathered_b = lax.optimization_barrier((plan_a, gathered_b))
    image_a = image_of(0, returned_of(plan_a))
    plan_b = planar_of(1, gathered_b)
    image = image_a + image_of(1, returned_of(plan_b))
    image = lax.all_to_all(
        image.astype(jnp.bfloat16), "line", split_axis=1, concat_axis=0, tiled=True
    ).astype(jnp.float32)
    summed = image
    ycoord = jnp.arange(obj_len, dtype=jnp.int32)
    inside = (ycoord[None, None, :] >= support_lo[:, :, None]) & (
        ycoord[None, None, :] < support_hi[:, :, None]
    )
    return jnp.where(inside & (summed > 0.0), summed, jnp.float32(0.0))


def solution(mesh):
    in_specs = (
        P("slab", "line", None),
        P("slab", "line"),
        P("slab", "line"),
        P(None, None, None, ("slab", "line"), None, None),
        P(),
        P(),
    )
    out_specs = P("slab", "line", None)
    return jax.shard_map(shards, mesh=mesh, in_specs=in_specs, out_specs=out_specs, check_vma=False)
```

```python
import math

import jax
import jax.numpy as jnp
from jax import lax
from jax.sharding import PartitionSpec as P

N = 512


def phase_table(left_int, right_int, period):
    product = jnp.mod(left_int * right_int, period)
    angle = product.astype(jnp.float32) * (2.0 * math.pi / period)
    factor = 1.0 / math.sqrt(N)
    return (
        (jnp.cos(angle) * factor).astype(jnp.bfloat16),
        (jnp.sin(angle) * factor).astype(jnp.bfloat16),
    )


def contract(form, left_op, right_op):
    return jnp.einsum(form, left_op, right_op, preferred_element_type=jnp.float32)


def shards(estimate, support_lo, support_hi, measured, blocks, wedge):
    slab_count = lax.axis_size("slab")
    line_count = lax.axis_size("line")
    slab_index = lax.axis_index("slab")
    line_index = lax.axis_index("line")
    plane_rows, row_count, obj_len = estimate.shape
    half_freq = N // 2
    device_count = slab_count * line_count
    per_device = N // device_count
    cell_coord = jnp.arange(obj_len, dtype=jnp.int32) - obj_len // 2
    own_freq = (slab_index * line_count + line_index) * per_device + jnp.arange(
        per_device, dtype=jnp.int32
    )
    all_freq = jnp.arange(N, dtype=jnp.int32) - half_freq
    dft_cos, dft_sin = lax.optimization_barrier(
        phase_table(all_freq[:, None], cell_coord[None, :], N)
    )
    frac_rows = (2 * (own_freq - half_freq))[:, None, None] * all_freq[None, :, None]

    cells = estimate.astype(jnp.bfloat16)
    planes = lax.all_to_all(cells, "line", split_axis=0, concat_axis=1, tiled=True)
    forward_forms = ("kx,zxy->kzy", "ky,zxy->kzx")
    backward_forms = ("kx,kzy->zxy", "ky,kzx->zxy")
    block_len = measured.shape[-1]
    nblocks = N // block_len
    low_end = jnp.minimum(wedge[0], wedge[1])
    high_end = jnp.maximum(wedge[0], wedge[1])
    line_pos = jnp.arange(N, dtype=jnp.int32)
    excluded = ((line_pos >= low_end) & (line_pos < high_end)).reshape(nblocks, block_len)
    kweight = (jnp.abs(own_freq - half_freq).astype(jnp.float32) + 1.0) / half_freq
    measured_t = jnp.transpose(measured, (3, 0, 1, 4, 2, 5))

    def substitute(polar, group, part):
        m0 = measured_t[:, group, part, 0]
        m1 = measured_t[:, group, part, 1]
        first_of = blocks[:, group, 0][None, :, None]
        second_of = blocks[:, group, 1][None, :, None]
        chunks = []
        for nb in range(nblocks):
            hit0 = first_of == nb
            hit1 = second_of == nb
            use = (hit0 | hit1) & (~excluded[nb])[None, None, :]
            picked = jnp.where(hit0, m0, m1).astype(jnp.float32)
            chunks.append(
                jnp.where(use, picked, polar[..., nb * block_len : (nb + 1) * block_len])
            )
        value = jnp.concatenate(chunks, axis=-1) * kweight[:, None, None]
        return value.astype(jnp.bfloat16)

    def spectrum_of(group):
        real = contract(forward_forms[group], dft_cos, planes)
        imag = -contract(forward_forms[group], dft_sin, planes)
        return jnp.stack([real, imag]).astype(jnp.bfloat16)

    def exchange(spectrum):
        return lax.all_to_all(
            spectrum, ("slab", "line"), split_axis=1, concat_axis=2, tiled=True
        )

    def planar_of(group, gathered):
        pen_re = (
            contract("az,kzc->kac", dft_cos, gathered[0])
            + contract("az,kzc->kac", dft_sin, gathered[1])
        ).astype(jnp.bfloat16)
        pen_im = (
            contract("az,kzc->kac", dft_cos, gathered[1])
            - contract("az,kzc->kac", dft_sin, gathered[0])
        ).astype(jnp.bfloat16)
        polar_re = contract("klc,kac->kal", frac_cos, pen_re) + contract(
            "klc,kac->kal", frac_sin, pen_im
        )
        polar_im = contract("klc,kac->kal", frac_cos, pen_im) - contract(
            "klc,kac->kal", frac_sin, pen_re
        )
        weighted_re = substitute(polar_re, group, 0)
        weighted_im = substitute(polar_im, group, 1)
        adj_re = (
            contract("klc,kal->kac", frac_cos, weighted_re)
            - contract("klc,kal->kac", frac_sin, weighted_im)
        ).astype(jnp.bfloat16)
        adj_im = (
            contract("klc,kal->kac", frac_cos, weighted_im)
            + contract("klc,kal->kac", frac_sin, weighted_re)
        ).astype(jnp.bfloat16)
        plan_re = (
            contract("az,kac->kzc", dft_cos, adj_re) - contract("az,kac->kzc", dft_sin, adj_im)
        ).astype(jnp.bfloat16)
        plan_im = (
            contract("az,kac->kzc", dft_cos, adj_im) + contract("az,kac->kzc", dft_sin, adj_re)
        ).astype(jnp.bfloat16)
        return jnp.stack([plan_re, plan_im])

    def image_of(group, returned):
        return contract(backward_forms[group], dft_cos, returned[0]) - contract(
            backward_forms[group], dft_sin, returned[1]
        )

    spectra = jnp.stack([spectrum_of(0), spectrum_of(1)])
    spectra, frac_rows = lax.optimization_barrier((spectra, frac_rows))
    frac_cos, frac_sin = lax.optimization_barrier(
        phase_table(frac_rows, cell_coord[None, None, :], N * N)
    )
    gathered = lax.all_to_all(spectra, ("slab", "line"), split_axis=2, concat_axis=3, tiled=True)
    gathered_a, gathered_b = gathered[0], gathered[1]
    plans = jnp.stack([planar_of(0, gathered_a), planar_of(1, gathered_b)])
    returned = lax.all_to_all(plans, ("slab", "line"), split_axis=3, concat_axis=2, tiled=True)
    image = image_of(0, returned[0]) + image_of(1, returned[1])
    image = lax.all_to_all(
        image.astype(jnp.bfloat16), "line", split_axis=1, concat_axis=0, tiled=True
    ).astype(jnp.float32)
    summed = image
    ycoord = jnp.arange(obj_len, dtype=jnp.int32)
    inside = (ycoord[None, None, :] >= support_lo[:, :, None]) & (
        ycoord[None, None, :] < support_hi[:, :, None]
    )
    return jnp.where(inside & (summed > 0.0), summed, jnp.float32(0.0))


def solution(mesh):
    in_specs = (
        P("slab", "line", None),
        P("slab", "line"),
        P("slab", "line"),
        P(None, None, None, ("slab", "line"), None, None),
        P(),
        P(),
    )
    out_specs = P("slab", "line", None)
    return jax.shard_map(shards, mesh=mesh, in_specs=in_specs, out_specs=out_specs, check_vma=False)
```

```python
import math

import jax
import jax.numpy as jnp
from jax import lax
from jax.sharding import PartitionSpec as P

N = 512


def phase_table(left_int, right_int, period):
    product = jnp.mod(left_int * right_int, period)
    angle = product.astype(jnp.float32) * (2.0 * math.pi / period)
    factor = 1.0 / math.sqrt(N)
    return (
        (jnp.cos(angle) * factor).astype(jnp.bfloat16),
        (jnp.sin(angle) * factor).astype(jnp.bfloat16),
    )


def contract(form, left_op, right_op):
    return jnp.einsum(form, left_op, right_op, preferred_element_type=jnp.float32)


def shards(estimate, support_lo, support_hi, measured, blocks, wedge):
    slab_count = lax.axis_size("slab")
    line_count = lax.axis_size("line")
    slab_index = lax.axis_index("slab")
    line_index = lax.axis_index("line")
    plane_rows, row_count, obj_len = estimate.shape
    half_freq = N // 2
    device_count = slab_count * line_count
    per_device = N // device_count
    cell_coord = jnp.arange(obj_len, dtype=jnp.int32) - obj_len // 2
    own_freq = (slab_index * line_count + line_index) * per_device + jnp.arange(
        per_device, dtype=jnp.int32
    )
    all_freq = jnp.arange(N, dtype=jnp.int32) - half_freq
    dft_cos, dft_sin = lax.optimization_barrier(
        phase_table(all_freq[:, None], cell_coord[None, :], N)
    )
    frac_rows = (2 * (own_freq - half_freq))[:, None, None] * all_freq[None, :, None]

    cells = estimate.astype(jnp.bfloat16)
    planes = lax.all_to_all(cells, "line", split_axis=0, concat_axis=1, tiled=True)
    forward_forms = ("kx,zxy->kzy", "ky,zxy->kzx")
    backward_forms = ("kx,kzy->zxy", "ky,kzx->zxy")
    block_len = measured.shape[-1]
    nblocks = N // block_len
    low_end = jnp.minimum(wedge[0], wedge[1])
    high_end = jnp.maximum(wedge[0], wedge[1])
    line_pos = jnp.arange(N, dtype=jnp.int32)
    excluded = ((line_pos >= low_end) & (line_pos < high_end)).reshape(nblocks, block_len)
    kweight = (jnp.abs(own_freq - half_freq).astype(jnp.float32) + 1.0) / half_freq
    measured_t = jnp.transpose(measured, (3, 0, 1, 4, 2, 5))

    def substitute(polar, group, part):
        m0 = measured_t[:, group, part, 0]
        m1 = measured_t[:, group, part, 1]
        first_of = blocks[:, group, 0][None, :, None]
        second_of = blocks[:, group, 1][None, :, None]
        chunks = []
        for nb in range(nblocks):
            hit0 = first_of == nb
            hit1 = second_of == nb
            use = (hit0 | hit1) & (~excluded[nb])[None, None, :]
            picked = jnp.where(hit0, m0, m1).astype(jnp.float32)
            chunks.append(
                jnp.where(use, picked, polar[..., nb * block_len : (nb + 1) * block_len])
            )
        value = jnp.concatenate(chunks, axis=-1) * kweight[:, None, None]
        return value.astype(jnp.bfloat16)

    def spectrum_of(group):
        real = contract(forward_forms[group], dft_cos, planes)
        imag = -contract(forward_forms[group], dft_sin, planes)
        return jnp.stack([real, imag]).astype(jnp.bfloat16)

    def exchange(spectrum):
        return lax.all_to_all(
            spectrum, ("slab", "line"), split_axis=1, concat_axis=2, tiled=True
        )

    def planar_of(group, gathered):
        pen_re = (
            contract("az,kzc->kac", dft_cos, gathered[0])
            + contract("az,kzc->kac", dft_sin, gathered[1])
        ).astype(jnp.bfloat16)
        pen_im = (
            contract("az,kzc->kac", dft_cos, gathered[1])
            - contract("az,kzc->kac", dft_sin, gathered[0])
        ).astype(jnp.bfloat16)
        polar_re = contract("klc,kac->kal", frac_cos, pen_re) + contract(
            "klc,kac->kal", frac_sin, pen_im
        )
        polar_im = contract("klc,kac->kal", frac_cos, pen_im) - contract(
            "klc,kac->kal", frac_sin, pen_re
        )
        weighted_re = substitute(polar_re, group, 0)
        weighted_im = substitute(polar_im, group, 1)
        adj_re = (
            contract("klc,kal->kac", frac_cos, weighted_re)
            - contract("klc,kal->kac", frac_sin, weighted_im)
        ).astype(jnp.bfloat16)
        adj_im = (
            contract("klc,kal->kac", frac_cos, weighted_im)
            + contract("klc,kal->kac", frac_sin, weighted_re)
        ).astype(jnp.bfloat16)
        plan_re = (
            contract("az,kac->kzc", dft_cos, adj_re) - contract("az,kac->kzc", dft_sin, adj_im)
        ).astype(jnp.bfloat16)
        plan_im = (
            contract("az,kac->kzc", dft_cos, adj_im) + contract("az,kac->kzc", dft_sin, adj_re)
        ).astype(jnp.bfloat16)
        return jnp.stack([plan_re, plan_im])

    def returned_of(plan):
        return lax.all_to_all(plan, ("slab", "line"), split_axis=2, concat_axis=1, tiled=True)

    def image_of(group, returned):
        return contract(backward_forms[group], dft_cos, returned[0]) - contract(
            backward_forms[group], dft_sin, returned[1]
        )

    spectra = jnp.stack([spectrum_of(0), spectrum_of(1)])
    spectra, frac_rows = lax.optimization_barrier((spectra, frac_rows))
    frac_cos, frac_sin = lax.optimization_barrier(
        phase_table(frac_rows, cell_coord[None, None, :], N * N)
    )
    gathered = lax.all_to_all(spectra, ("slab", "line"), split_axis=2, concat_axis=3, tiled=True)
    plan_a = planar_of(0, gathered[0])
    plan_a, gathered = lax.optimization_barrier((plan_a, gathered))
    gathered_b = gathered[1]
    image_a = image_of(0, returned_of(plan_a))
    plan_b = planar_of(1, gathered_b)
    image = image_a + image_of(1, returned_of(plan_b))
    image = lax.all_to_all(
        image.astype(jnp.bfloat16), "line", split_axis=1, concat_axis=0, tiled=True
    ).astype(jnp.float32)
    summed = image
    ycoord = jnp.arange(obj_len, dtype=jnp.int32)
    inside = (ycoord[None, None, :] >= support_lo[:, :, None]) & (
        ycoord[None, None, :] < support_hi[:, :, None]
    )
    return jnp.where(inside & (summed > 0.0), summed, jnp.float32(0.0))


def solution(mesh):
    in_specs = (
        P("slab", "line", None),
        P("slab", "line"),
        P("slab", "line"),
        P(None, None, None, ("slab", "line"), None, None),
        P(),
        P(),
    )
    out_specs = P("slab", "line", None)
    return jax.shard_map(shards, mesh=mesh, in_specs=in_specs, out_specs=out_specs, check_vma=False)
```
